256 devices in a mesh: ctx: 32 (over x, y, z_lo), tp: 8 (over z_hi, core).
Axes of the slice: x: 4, y: 4, z: 8 (z_hi: 4, z_lo: 2; z = z_hi * 2 + z_lo), core: 2. Of those that a mesh axis runs over, the one named last changes fastest.
Arguments:
- features: bfloat16 [8192, 8192], P('ctx', 'tp'), may hold values from -6 to 6
- inner: bfloat16 [8192, 8192], P('ctx', 'tp'), may hold values from -6 to 6
- w_bc: bfloat16 [8192, 2, 1024], P('ctx', None, 'tp'), may hold values from -0.005859375 to 0.005859375
- w_dt: bfloat16 [8192, 128], P('ctx', 'tp'), may hold values from -0.0625 to 0.0625
- dt_bias: float32 [128], P('tp'), may hold values from -4 to 0
- decay_rate: float32 [128], P('tp'), may hold values from 0.00012207031 to 1
- skip: float32 [128], P('tp'), may hold values from 0.5 to 1.5
- cotangent: bfloat16 [8192, 8192], P('ctx', 'tp'), may hold values from -6 to 6
- fisher: float32 [8192, 2, 1024], P('ctx', None, 'tp'), may hold values from 0.5 to 4
- importance: float32 [8192, 2, 1024], P('ctx', None, 'tp'), may hold values from 0 to 10
Outputs:
- outputs: bfloat16 [8192, 8192], P('ctx', 'tp')
- grad_inner: bfloat16 [8192, 8192], P('ctx', 'tp')
- grad_features: bfloat16 [8192, 8192], P('ctx', 'tp')
- weight_new: float32 [8192, 2, 1024], P('ctx', None, 'tp')
- fisher_new: float32 [8192, 2, 1024], P('ctx', None, 'tp')
- importance_new: float32 [8192, 2, 1024], P('ctx', None, 'tp')
The draws below stay inside these ranges and needn't reach their ends.
All inputs are finite; a program needn't handle non-finite values.
Results may differ from the reference program's by a relative error of at most 0.014.
Values may be sent and summed in bfloat16 or wider, within the bound.
A program may use at most 128 MiB of HBM per device.

```python
import math
from functools import partial
import jax
import jax.numpy as jnp
from jax import lax

D = 8192
HEADS = 128
P_SIZE = 64
N = 128
G = 8
SPAN = 256
TOKENS = 8192


def shard_levels(own_key, dims, shards, least, high):
    level = 1.0
    for axis_at, blocks in shards:
        heights = jax.random.uniform(jax.random.fold_in(jax.random.fold_in(own_key, 6), axis_at), (blocks,), jnp.float32, least / len(shards), high / len(shards))
        level = level * jnp.repeat(jnp.exp(heights), dims[axis_at] // blocks).reshape((-1,) + (1,) * (len(dims) - 1 - axis_at))
    return level


def scatter_about(own_key, dims, spread, limit, pieces=(), held_as=jnp.bfloat16):
    values = jax.random.normal(own_key, dims, jnp.float32) * spread
    if len(pieces) > 0:
        values = shard_levels(own_key, dims, pieces, -0.22, 0.18) * values
    return jnp.clip(values, min=-limit, max=limit).astype(held_as)


def setup_inputs(seed: int = 0) -> dict:
    arg_keys = jax.random.split(jax.random.key(seed), 11)
    return {
        "features": scatter_about(arg_keys[0], (TOKENS, D), 1.0, 6.0, ((0, 32), (1, 8))),
        "inner": scatter_about(arg_keys[1], (TOKENS, HEADS * P_SIZE), 1.0, 6.0, ((0, 32), (1, 8))),
        "w_bc": scatter_about(arg_keys[2], (D, 2, G * N), (D * N) ** -0.5, 0.005859375, ((0, 32), (2, 8))),
        "w_dt": scatter_about(arg_keys[3], (D, HEADS), D ** -0.5, 0.0625, ((0, 32), (1, 8))),
        "dt_bias": jnp.clip(-4.0 + 4.0 * jax.random.uniform(arg_keys[4], (HEADS,), jnp.float32) ** shard_levels(arg_keys[4], (HEADS,), ((0, 8),), -0.2, 0.2), -4.0, 0.0),
        "decay_rate": jnp.clip(jnp.exp(math.log(1.0) - 9.010913 * jax.random.uniform(arg_keys[5], (HEADS,), jnp.float32) ** shard_levels(arg_keys[5], (HEADS,), ((0, 8),), -0.2, 0.2)), 0.00012207031, 1.0),
        "skip": jnp.clip(0.5 + 1.0 * jax.random.uniform(arg_keys[6], (HEADS,), jnp.float32) ** shard_levels(arg_keys[6], (HEADS,), ((0, 8),), -0.2, 0.2), 0.5, 1.5),
        "cotangent": scatter_about(arg_keys[7], (TOKENS, HEADS * P_SIZE), 1.0, 6.0, ((0, 32), (1, 8))),
        "fisher": jnp.clip(jnp.exp(math.log(4.0) - 2.0794415 * jax.random.uniform(arg_keys[8], (D, 2, G * N), jnp.float32) ** shard_levels(arg_keys[8], (D, 2, G * N), ((0, 32), (2, 8)), -0.2, 0.2)), 0.5, 4.0),
        "importance": jnp.clip(10.0 * jax.random.uniform(arg_keys[9], (D, 2, G * N), jnp.float32) ** shard_levels(arg_keys[9], (D, 2, G * N), ((0, 32), (2, 8)), -0.2, 0.2), 0.0, 10.0),
    }


HIGH = lax.Precision.HIGHEST
MIX = 0.25
STEP = 0.1
EPS = 1e-06

def span_pass(dt_bias, rate, state, blocks):
    xc, bc, cc, zc = blocks
    dt = jax.nn.softplus(zc + dt_bias)
    logs = -rate * dt
    cums = jnp.cumsum(logs, axis=0)
    length = xc.shape[0]
    rows = lax.broadcasted_iota(jnp.int32, (length, length), 0)
    cols = lax.broadcasted_iota(jnp.int32, (length, length), 1)
    causal = rows >= cols
    scores = jnp.einsum('ign,jgn->gij', cc, bc, precision=HIGH)
    order = jnp.transpose(cums, (1, 2, 0))
    diff = order[:, :, :, None] - order[:, :, None, :]
    decays = jnp.where(causal, jnp.exp(jnp.where(causal, diff, 0.0)), 0.0)
    weights = decays * scores[:, None] * jnp.transpose(dt, (1, 2, 0))[:, :, None, :]
    intra = jnp.einsum('ghij,jghp->ighp', weights, xc, precision=HIGH)
    inter = jnp.exp(cums)[..., None] * jnp.einsum('ign,ghpn->ighp', cc, state, precision=HIGH)
    last = cums[-1]
    tail = jnp.exp(last[None] - cums) * dt
    fresh = jnp.einsum('jghp,jgh,jgn->ghpn', xc, tail, bc, precision=HIGH)
    new_state = jnp.exp(last)[..., None, None] * state + fresh
    return (new_state, intra + inter)

def run_spans(x, b, c, z, dt_bias, rate):
    tokens, groups, heads, width = x.shape
    count = tokens // SPAN
    state0 = jnp.zeros((groups, heads, width, b.shape[-1]), jnp.float32)
    blocks = (x.reshape(count, SPAN, groups, heads, width), b.reshape(count, SPAN, groups, b.shape[-1]), c.reshape(count, SPAN, groups, c.shape[-1]), z.reshape(count, SPAN, groups, heads))
    final, ys = lax.scan(partial(span_pass, dt_bias, rate), state0, blocks)
    return (ys.reshape(tokens, groups, heads, width), final)

def rwalk(weight, grad, fisher, importance):
    fisher_new = MIX * grad * grad + (1.0 - MIX) * fisher
    delta = -STEP * grad
    importance_new = importance + -grad * delta / (0.5 * fisher_new * delta * delta + EPS)
    weight_new = weight.astype(jnp.float32) + delta
    return (weight_new, fisher_new, importance_new)

def reference(features, inner, w_bc, w_dt, dt_bias, decay_rate, skip, cotangent, fisher, importance):
    tokens = features.shape[0]
    per_group = HEADS // G
    wide = w_bc.reshape(D, 2 * G * N)
    proj = jnp.dot(features, wide, preferred_element_type=jnp.float32)
    proj = lax.optimization_barrier(proj.astype(jnp.bfloat16)).astype(jnp.float32)
    bmat = proj[:, :G * N].reshape(tokens, G, N)
    cmat = proj[:, G * N:].reshape(tokens, G, N)
    zdt = jnp.dot(features, w_dt, preferred_element_type=jnp.float32).reshape(tokens, G, per_group)
    bias = dt_bias.reshape(G, per_group)
    rate = decay_rate.reshape(G, per_group)
    gain = skip.reshape(G, per_group)
    xval = inner.astype(jnp.float32).reshape(tokens, G, per_group, P_SIZE)

    def layer(xv, bv, cv, zv):
        core, final = run_spans(xv, bv, cv, zv, bias, rate)
        return core + gain[..., None] * xv
    out, back = jax.vjp(layer, xval, bmat, cmat, zdt)
    dx, dbm, dcm, dz = back(cotangent.astype(jnp.float32).reshape(tokens, G, per_group, P_SIZE))
    outputs = out.reshape(tokens, HEADS * P_SIZE).astype(jnp.bfloat16)
    grad_inner = dx.reshape(tokens, HEADS * P_SIZE).astype(jnp.bfloat16)
    dproj = jnp.concatenate([dbm.reshape(tokens, G * N), dcm.reshape(tokens, G * N)], axis=1).astype(jnp.bfloat16)
    dz_half = dz.reshape(tokens, HEADS).astype(jnp.bfloat16)
    grad_features = lax.dot_general(dproj, wide, (((1,), (1,)), ((), ())), preferred_element_type=jnp.float32) + lax.dot_general(dz_half, w_dt, (((1,), (1,)), ((), ())), preferred_element_type=jnp.float32)
    grad_features = grad_features.astype(jnp.bfloat16)
    summed = lax.dot_general(features, dproj, (((0,), (0,)), ((), ())), preferred_element_type=jnp.float32)
    grad = summed.reshape(D, 2, G * N) / tokens
    weight_new, fisher_new, importance_new = rwalk(w_bc, grad, fisher, importance)
    return (outputs, grad_inner, grad_features, weight_new, fisher_new, importance_new)
```

```python
from functools import partial

import jax
import jax.numpy as jnp
from jax import lax
from jax.experimental import pallas as pl
from jax.experimental.pallas import tpu as pltpu
from jax.sharding import Mesh
from jax.sharding import PartitionSpec as P

AXES = ("x", "y", "zl", "zh", "core")
CTX = AXES[:3]
TP = AXES[3:]
DEPTH = 8192
TOKENS = 8192
HEADS = 16
WIDTH = 64
N = 128
SPAN = 256
SPANS = 32
MSG = 272
SLICE = 32
MIX = 0.25
STEP = 0.1
EPS = 1e-06
MESH = pl.DeviceIdType.MESH
BF = jnp.bfloat16
F32 = jnp.float32
HIGH = lax.Precision.HIGHEST
VMEM = pl.BlockSpec(memory_space=pltpu.VMEM)
ANY = pl.BlockSpec(memory_space=pl.ANY)


def place():
    return tuple(lax.axis_index(a) for a in AXES)


def at(x, y, zl, zh, core):
    return {"x": x, "y": y, "zl": zl, "zh": zh, "core": core}


def spread_to(x, y, zl, zh, core):
    return at((x - zh + 4) % 4, 2 * (y % 2) + zl, 1 - core, x, y // 2)


def spread_from(x, y, zl, zh, core):
    return at(zh, 2 * core + y // 2, y % 2, (zh - x + 4) % 4, 1 - zl)


def greet(sources):
    barrier = pltpu.get_barrier_semaphore()
    for device in sources:
        pl.semaphore_signal(barrier, inc=1, device_id=device, device_id_type=MESH)
    return lambda: pl.semaphore_wait(barrier, len(sources))


def remote(src, dst, send, recv, device):
    return pltpu.make_async_remote_copy(
        src_ref=src,
        dst_ref=dst,
        send_sem=send,
        recv_sem=recv,
        device_id=device,
        device_id_type=MESH,
    )


def dot(a, b, dims=((1,), (0,)), precision=None):
    return lax.dot_general(a, b, (dims, ((), ())), precision=precision, preferred_element_type=F32)


NT = ((1,), (1,))
TN = ((0,), (0,))


def wide(rows):
    cols = rows.T
    return jnp.concatenate(
        [jnp.broadcast_to(cols[:, h : h + 1], (SPAN, WIDTH)) for h in range(HEADS)], axis=1
    )


def by_head():
    row = lax.broadcasted_iota(jnp.int32, (HEADS, HEADS * WIDTH), 0)
    col = lax.broadcasted_iota(jnp.int32, (HEADS, HEADS * WIDTH), 1)
    return jnp.where(col // WIDTH == row, 1.0, 0.0)


def step_sizes(z, bias, rate):
    dt = jax.nn.softplus(z + bias)
    row = lax.broadcasted_iota(jnp.int32, (SPAN, SPAN), 0)
    col = lax.broadcasted_iota(jnp.int32, (SPAN, SPAN), 1)
    upto = jnp.where(row <= col, 1.0, 0.0)
    cums = dot(-rate * dt, upto, precision=HIGH)
    return dt, cums


PIECES = (("x", 0, 48, 80), ("y", 80, 112, 144), ("x", 144, 176, 208), ("y", 208, 240, MSG))
STEPS = sorted(
    ((i, j, k) for i in range(4) for j in range(4) for k in range(2) if i + j + k > 0),
    key=lambda s: -(min(s[0], 4 - s[0]) + min(s[1], 4 - s[1]) + s[2]),
)
NEAR = (0, -1, 1, 2)
EARLY = True
FAR = (2, 1, -1, 0)


def layer_kernel(
    w_hbm,
    wd_ref,
    f_ref,
    x_hbm,
    u_hbm,
    bias_hbm,
    rate_hbm,
    skip_hbm,
    y_hbm,
    dx_hbm,
    gf_hbm,
    grad_ref,
    w_ref,
    bias_ref,
    rate_ref,
    skip_ref,
    rows32,
    f2t,
    gf32,
    gf_ref,
    block,
    x_ref,
    u_ref,
    y_ref,
    dx_ref,
    wt,
    f2,
    kept,
    given,
    taken,
    both,
    r_in,
    msg,
    got,
    out,
    hg,
    ysum,
    esum,
    d_out,
    dp,
    gr,
    r1x,
    r1y,
    acc,
    r2,
    done,
    gf_out,
    gf_in,
    a_send,
    a_recv,
    b_send,
    b_recv,
    c_send,
    c_recv,
    d_send,
    d_recv,
    e_send,
    e_recv,
    local_sem,
    plane_sem,
):
    me = place()
    x, y, zl, zh, core = me
    ring = {"x": x, "y": y}
    span = x * 8 + y * 2 + zl
    partner = {"core": 1 - core}
    beside = {"zl": 1 - zl}
    started = []

    def by(axis, step):
        return {axis: (ring[axis] + step + 4) % 4}

    def span_at(step, sign):
        i, j, k = step
        to = ((x + sign * i + 4) % 4, (y + sign * j + 4) % 4, (zl + k) % 2)
        return to[0] * 8 + to[1] * 2 + to[2], dict(zip(CTX, to))

    def start(copy):
        copy.start()
        started.append(copy)
        return copy

    met = greet(
        [spread_from(*me), beside, by("x", 1), by("x", 3), by("y", 1), by("y", 3), partner]
        + [{"zh": (zh + e) % 4, "zl": 1 - core, "core": zl} for e in range(4)]
    )
    pairs = (
        (w_hbm, w_ref),
        (f_ref, f2.at[zl]),
        (x_hbm, x_ref),
        (u_hbm, u_ref),
        (bias_hbm, bias_ref),
        (rate_hbm, rate_ref),
        (skip_hbm, skip_ref),
    )
    loads = [
        pltpu.make_async_copy(src, dst, local_sem.at[k]) for k, (src, dst) in enumerate(pairs)
    ]
    for copy in loads:
        copy.start()
    loads[0].wait()
    rows32[...] = w_ref[...].astype(F32)
    block[:, :N] = rows32[pl.ds(0, 256, stride=2), :].astype(BF)
    block[:, N:] = rows32[pl.ds(1, 256, stride=2), :].astype(BF)
    met()

    index = {}

    def message(key, block, axis, step):
        k = index.setdefault(key, len(index))
        return remote(block, block, a_send.at[k], a_recv.at[k], by(axis, step))

    def slot(p, a, b, part=0):
        first, lo, mid, hi = PIECES[p]
        lo, hi = ((lo, hi), (lo, mid), (mid, hi))[part]
        i, j = (a, b) if first == "x" else (b, a)
        return wt.at[(x + i + 4) % 4, (y + j + 4) % 4, pl.ds(lo, hi - lo), :]

    def axes(p):
        return ("x", "y") if PIECES[p][0] == "x" else ("y", "x")

    def part_of(step):
        return 1 if step == 1 else 2

    def along(p, d):
        for step in (1, -1):
            start(message(("b", p, d, step), slot(p, d, 0), axes(p)[1], step))

    def along_more(p, d):
        second = axes(p)[1]
        for step in (1, -1):
            message(("b", p, d, step), slot(p, d, -step), second, step).wait_recv()
            start(message(("br", p, d, step), slot(p, d, -step, part_of(step)), second, step))

    def along_end(p, d):
        for step in (1, -1):
            block = slot(p, d, -2 * step, part_of(step))
            message(("br", p, d, step), block, axes(p)[1], step).wait_recv()

    to = spread_to(*me)

    def move(p, here):
        _, lo, _, hi = PIECES[p]
        hi = min(hi, 256)
        dst = wt.at[here[0], here[1], pl.ds(lo, hi - lo)]
        return remote(block.at[pl.ds(lo, hi - lo)], dst, e_send.at[p], e_recv.at[p], to)

    def move_steps(here):
        dst = wt.at[here[0], here[1], pl.ds(256, 16)]
        return remote(wd_ref, dst, e_send.at[5], e_recv.at[5], to)

    every = range(len(PIECES))
    for p in every:
        start(move(p, (to["x"], to["y"])))
    start(move_steps((to["x"], to["y"])))
    swap = remote(f_ref, f2.at[zl], e_send.at[4], e_recv.at[4], beside)
    if EARLY:
        start(swap)
    for p in every:
        move(p, (x, y)).wait_recv()
        if p == every[-1]:
            move_steps((x, y)).wait_recv()
        for step in (1, -1):
            start(message(("a", p, step), slot(p, 0, 0), axes(p)[0], step))
        along(p, 0)
    if not EARLY:
        start(swap)
    lead = [p for p in every if PIECES[p][0] == "x"]
    trail = [p for p in every if PIECES[p][0] == "y"]
    for step in (1, -1):
        for p in every:
            message(("a", p, step), slot(p, -step, 0), axes(p)[0], step).wait_recv()
            start(
                message(("ar", p, step), slot(p, -step, 0, part_of(step)), axes(p)[0], step)
            )
            along(p, -step)
    for p in every:
        along_more(p, 0)
    for p in every:
        for step in (1, -1):
            block = slot(p, -2 * step, 0, part_of(step))
            message(("ar", p, step), block, axes(p)[0], step).wait_recv()
        along(p, 2)
    swaps = []

    def partial_product(i):
        a = (x + NEAR[i] + 4) % 4
        for which, ref in ((1 - core, given), (core, kept)):
            ref[i, 0:256, :] = dot(f2[which], wt[a, :, 0:256, :].reshape(1024, 256))
            ref[i, 256:MSG, :] = sum(
                dot(wt[a, r, 256:MSG, :], f2[which, :, 256 * r : 256 * (r + 1)], NT)
                for r in range(4)
            )
            if ref is given:
                swaps.append(
                    start(remote(given.at[i], taken.at[i], b_send.at[i], b_recv.at[i], partner))
                )

    def pass_on(i):
        swaps[i].wait_recv()
        both[i] = (kept[i] + taken[i]).astype(BF)
        group = (zh - x - NEAR[i] + 8) % 4
        target = {"zh": group, "zl": core, "core": 1 - zl}
        start(remote(both.at[i], r_in.at[i], b_send.at[4 + i], b_recv.at[4 + i], target))

    for p in every:
        along_more(p, -1)
    loads[1].wait()
    remote(f_ref, f2.at[1 - zl], e_send.at[4], e_recv.at[4], beside).wait_recv()
    for p in lead:
        along_end(p, 0)
    partial_product(0)
    for p in every:
        along_more(p, 1)
    for p in every:
        along_more(p, 2)
    pass_on(0)
    for i in (1, 2):
        for p in lead:
            along_end(p, NEAR[i])
        partial_product(i)
        if i == 2:
            pass_on(1)
    for p in lead:
        along_end(p, 2)
    for p in trail:
        for d in NEAR:
            along_end(p, d)
    pl.semaphore_signal(plane_sem, inc=1, device_id=beside, device_id_type=MESH)
    partial_product(3)
    pass_on(2)
    pass_on(3)
    for i in range(4):
        group = (zh - x - NEAR[i] + 8) % 4
        target = {"zh": group, "zl": core, "core": 1 - zl}
        remote(both.at[i], r_in.at[i], b_send.at[4 + i], b_recv.at[4 + i], target).wait_recv()

    proj = sum(r_in[k, 0:256, :].astype(F32) for k in range(4)).astype(BF)
    z = sum(r_in[k, 256:MSG, :].astype(F32) for k in range(4))
    bm, cm = proj[:, :N], proj[:, N:]
    for copy in loads[2:]:
        copy.wait()
    eye = lax.broadcasted_iota(jnp.int32, (HEADS, HEADS), 0)
    eye = eye == lax.broadcasted_iota(jnp.int32, (HEADS, HEADS), 1)

    def column(ref):
        rows = jnp.broadcast_to(ref[...], (HEADS, HEADS))
        return jnp.sum(jnp.where(eye, rows, 0.0), axis=1, keepdims=True)

    bias, rate, gain = column(bias_ref), column(rate_ref), column(skip_ref)
    dt, cums = step_sizes(z, bias, rate)
    last = cums[:, SPAN - 1 : SPAN]
    tail = jnp.exp(last - cums) * dt
    xt = (x_ref[...].astype(F32) * wide(tail)).astype(BF)
    ue = (u_ref[...].astype(F32) * wide(jnp.exp(cums))).astype(BF)
    fresh = dot(xt, bm, TN).astype(BF)
    back = dot(ue, cm, TN).astype(BF)
    decay = jnp.exp(last)
    first = decay.astype(BF).astype(F32)
    second = (decay - first).astype(BF).astype(F32)
    third = decay - first - second
    row16 = lax.broadcasted_iota(jnp.int32, (16, N), 0)
    for s in range(SPANS):
        h = s // 2
        rows = slice(SLICE * s, SLICE * (s + 1))
        msg[s, 0:32, :] = fresh[rows]
        msg[s, 32:64, :] = back[rows]
        pieces = [jnp.broadcast_to(v[h : h + 1, :], (16, N)) for v in (first, second, third)]
        msg[s, 64:80, :] = jnp.where(
            row16 == 0, pieces[0], jnp.where(row16 == 1, pieces[1], pieces[2])
        ).astype(BF)
    pl.semaphore_wait(plane_sem, 1)
    for d, step in enumerate(STEPS):
        p, there = span_at(step, 1)
        start(remote(msg.at[p], got.at[span], c_send.at[0, d], c_recv.at[0, d], there))
    got[span] = msg[span]

    for which in (0, 1):
        f2t[which] = f2[which].T
    scores = dot(cm, bm, NT)
    cols = cums.T
    row = lax.broadcasted_iota(jnp.int32, (SPAN, SPAN), 0)
    col = lax.broadcasted_iota(jnp.int32, (SPAN, SPAN), 1)
    causal = row >= col
    lane = lax.broadcasted_iota(jnp.int32, (SPAN, 2 * WIDTH), 1)
    zero = jnp.zeros((SPAN, 2 * WIDTH), BF)
    dt_cols = dt.T
    dscores = jnp.zeros((SPAN, SPAN), F32)
    for pair in range(HEADS // 2):
        cut = slice(2 * WIDTH * pair, 2 * WIDTH * (pair + 1))
        x2, u2 = x_ref[:, cut], u_ref[:, cut]
        steps = jnp.where(
            lane < WIDTH,
            jnp.broadcast_to(dt_cols[:, 2 * pair : 2 * pair + 1], (SPAN, 2 * WIDTH)),
            jnp.broadcast_to(dt_cols[:, 2 * pair + 1 : 2 * pair + 2], (SPAN, 2 * WIDTH)),
        )
        xd = (x2.astype(F32) * steps).astype(BF)
        y2 = e2 = None
        for k in range(2):
            h = 2 * pair + k
            mine = lane < WIDTH if k == 0 else lane >= WIDTH
            diff = cols[:, h : h + 1] - cums[h : h + 1, :]
            fall = jnp.where(causal, jnp.exp(jnp.minimum(diff, 0.0)), 0.0)
            a = (fall * scores).astype(BF)
            uh = jnp.where(mine, u2, zero)
            yk = dot(a, jnp.where(mine, xd, zero))
            ek = dot(a, uh, TN)
            y2 = yk if y2 is None else y2 + yk
            e2 = ek if e2 is None else e2 + ek
            dscores = dscores + (fall * dt[h : h + 1, :]) * dot(uh, x2, NT)
        ysum[:, cut] = y2
        esum[:, cut] = e2
    ds = dscores.astype(BF)

    for d, step in enumerate(STEPS):
        p, there = span_at(step, -1)
        remote(msg.at[p], got.at[p], c_send.at[0, d], c_recv.at[0, d], there).wait_recv()

    def decay_of(p):
        rows = got[p, 64:80, :].astype(F32)
        return rows[0:1] + rows[1:2] + rows[2:3]

    state = jnp.zeros((SLICE, N), F32)
    for p in range(SPANS):
        out[p, 0:32, :] = state.astype(BF)
        state = decay_of(p) * state + got[p, 0:32, :].astype(F32)
    state = jnp.zeros((SLICE, N), F32)
    for p in reversed(range(SPANS)):
        out[p, 32:64, :] = state.astype(BF)
        state = decay_of(p) * state + got[p, 32:64, :].astype(F32)
    for d, step in enumerate(STEPS):
        p, there = span_at(step, 1)
        start(remote(out.at[p], hg.at[span], c_send.at[1, d], c_recv.at[1, d], there))
    hg[span] = out[span]
    xf, uf = x_ref[...].astype(F32), u_ref[...].astype(F32)
    heads = by_head()
    e_in = esum[...]
    v_in = dot(heads, xf * e_in, NT, HIGH)
    dt_wide = wide(dt)
    grown = wide(jnp.exp(cums))
    left = wide(jnp.exp(last - cums))
    skip = jnp.concatenate(
        [jnp.broadcast_to(gain[h : h + 1, :], (SPAN, WIDTH)) for h in range(HEADS)], axis=1
    )
    from_here = jnp.where(row >= col, 1.0, 0.0)
    before = jnp.where(row < col, 1.0, 0.0)
    for d, step in enumerate(STEPS):
        p, there = span_at(step, -1)
        remote(out.at[p], hg.at[p], c_send.at[1, d], c_recv.at[1, d], there).wait_recv()

    enter = hg[:, 0:32, :].reshape(HEADS * WIDTH, N)
    leave = hg[:, 32:64, :].reshape(HEADS * WIDTH, N)
    d_out[0:256, N:] = (dot(ds, bm) + dot(ue, enter)).astype(BF)
    d_out[0:256, :N] = (dot(ds, cm, TN) + dot(xt, leave)).astype(BF)

    parts = (pl.ds(0, 256), pl.ds(256, 16))

    def share(i, part):
        a = (zh + x + FAR[i] + 4) % 4
        target = {"zh": a, "zl": 1 - core, "core": zl}
        rows, k = parts[part], 8 * part + i
        return remote(d_out.at[rows], dp.at[zl, i, rows], d_send.at[k], d_recv.at[k], target)

    def shared(i, part):
        a = (zh - x - FAR[i] + 8) % 4
        target = {"zh": a, "zl": 1 - core, "core": zl}
        rows, k = parts[part], 8 * part + i
        copy = remote(d_out.at[rows], dp.at[core, i, rows], d_send.at[k], d_recv.at[k], target)
        copy.wait_recv()

    def share_again(i, part, side):
        block, k = dp.at[side, i, parts[part]], 8 * part + 4 + i
        return remote(block, block, d_send.at[k], d_recv.at[k], partner)

    for i in range(4):
        start(share(i, 0))
    y_core = ysum[...] + grown * dot(cm, enter, NT)
    e_out = left * dot(bm, leave, NT)
    q = dot(heads, uf * y_core, NT, HIGH)
    v_out = dot(heads, xf * e_out, NT, HIGH)
    product = dot(heads, leave.astype(F32) * enter.astype(F32), precision=HIGH)
    product = decay * jnp.sum(product, axis=1, keepdims=True)
    dla = dot(q - dt * v_in, from_here, precision=HIGH)
    dla = dla + dot(dt * v_out, before, precision=HIGH) + product
    dz = (v_in + v_out - rate * dla) * jax.nn.sigmoid(z + bias)
    d_out[256:MSG, :] = dz.astype(BF)
    for i in range(4):
        start(share(i, 1))

    y_ref[...] = (y_core + skip * xf).astype(BF)
    dx_ref[...] = (dt_wide * (e_in + e_out) + skip * uf).astype(BF)
    stores = [
        pltpu.make_async_copy(src, dst, local_sem.at[7 + k])
        for k, (src, dst) in enumerate(((y_ref, y_hbm), (dx_ref, dx_hbm)))
    ]
    for copy in stores:
        copy.start()

    def sum_x(i, j):
        block = gr.at[i, (y + FAR[j] + 4) % 4, pl.ds(0, 128), :]
        k = 44 + 4 * i + j
        return remote(block, r1x.at[i, j], e_send.at[k], e_recv.at[k], by("x", FAR[i]))

    def sum_y(i, j):
        block = gr.at[i, (y + FAR[j] + 4) % 4, pl.ds(128, 128), :]
        k = 12 + 4 * i + j
        return remote(block, r1y.at[j, i], e_send.at[k], e_recv.at[k], by("y", FAR[j]))

    def weight_gradient(i):
        share_again(i, 0, 1 - core).wait_recv()
        mine = dot(f2t[0], dp[0, i, 0:256, :]) + dot(f2t[1], dp[1, i, 0:256, :])
        gr[i] = mine.reshape(4, 256, 256).astype(BF)
        if FAR[i] != 0:
            for j in range(4):
                start(sum_x(i, j))
        for j in range(3):
            start(sum_y(i, j))

    def feature_gradient(which, r, blocks):
        slots = [(x + FAR[i] + 4) % 4 for i in blocks]
        dzs = jnp.concatenate([dp[which, i, 256:MSG, :] for i in blocks], axis=0)
        rows = jnp.concatenate([wt[a, r, 256:MSG, :] for a in slots], axis=0)
        total = dot(dzs, rows, TN)
        for i, a in zip(blocks, slots):
            total = total + dot(dp[which, i, 0:256, :], wt[a, r, 0:256, :], NT)
        return total

    for i in range(4):
        shared(i, 0)
        start(share_again(i, 0, core))
        if i > 0:
            weight_gradient(i - 1)
    for i in range(4):
        shared(i, 1)
        start(share_again(i, 1, core))
    weight_gradient(3)
    for i in range(4):
        share_again(i, 1, 1 - core).wait_recv()

    def sum_again(half, j):
        axis = "y" if half == 0 else "x"
        block = acc.at[half, j]
        k = 32 + 4 * half + j
        return remote(block, r2.at[half, j], e_send.at[k], e_recv.at[k], by(axis, FAR[j]))

    backs = []
    for r in range(4):
        gf_out[r] = feature_gradient(1 - zl, r, (0, 1, 2, 3)).astype(BF)
        copy = remote(gf_out.at[r], gf_in.at[r], e_send.at[28 + r], e_recv.at[28 + r], beside)
        backs.append(start(copy))
    for j in range(4):
        total = gr[3, (y + FAR[j] + 4) % 4, 0:128, :].astype(F32)
        for i in range(3):
            sum_x(i, j).wait_recv()
            total = total + r1x[i, j].astype(F32)
        acc[0, j] = total.astype(BF)
        if j < 3:
            start(sum_again(0, j))
    for i in range(4):
        for j in range(3):
            sum_y(i, j).wait_recv()
        total = gr[i, y, 128:256, :].astype(F32)
        for j in range(3):
            total = total + r1y[j, i].astype(F32)
        acc[1, i] = total.astype(BF)
        if i < 3:
            start(sum_again(1, i))
    for r in range(4):
        gf32[r] = feature_gradient(zl, r, (0, 1, 2, 3))
    homes = []
    for half in (0, 1):
        total = acc[half, 3].astype(F32)
        for j in (1, 2, 0):
            sum_again(half, j).wait_recv()
            total = total + r2[half, j].astype(F32)
        done[half] = total.astype(BF)
        copy = remote(
            done.at[half],
            grad_ref.at[half],
            e_send.at[40 + half],
            e_recv.at[40 + half],
            spread_from(*me),
        )
        homes.append(start(copy))
    for r in range(4):
        backs[r].wait_recv()
        gf_ref[r] = (gf32[r] + gf_in[r].astype(F32)).astype(BF)
        part = gf_hbm.at[:, pl.ds(256 * r, 256)]
        stores.append(pltpu.make_async_copy(gf_ref.at[r], part, local_sem.at[9 + r]))
        stores[-1].start()
    for copy in homes:
        copy.wait_recv()
    for copy in started:
        copy.wait_send()
    for copy in stores:
        copy.wait()


def layer(rows, steps, features, x, u, bias, rate, skip):
    dma = pltpu.SemaphoreType.DMA
    return pl.pallas_call(
        layer_kernel,
        name="layer",
        out_shape=(
            jax.ShapeDtypeStruct((SPAN, 1024), BF),
            jax.ShapeDtypeStruct((SPAN, 1024), BF),
            jax.ShapeDtypeStruct((SPAN, 1024), BF),
            jax.ShapeDtypeStruct((2, 128, 256), BF),
        ),
        in_specs=[ANY] * 8,
        out_specs=(ANY, ANY, ANY, VMEM),
        scratch_shapes=[
            pltpu.VMEM((512, N), BF),
            pltpu.VMEM((1, HEADS), F32),
            pltpu.VMEM((1, HEADS), F32),
            pltpu.VMEM((1, HEADS), F32),
            pltpu.VMEM((512, N), F32),
            pltpu.VMEM((2, 1024, SPAN), BF),
            pltpu.VMEM((4, SPAN, 256), F32),
            pltpu.VMEM((4, SPAN, 256), BF),
            pltpu.VMEM((256, 256), BF),
            pltpu.VMEM((SPAN, 1024), BF),
            pltpu.VMEM((SPAN, 1024), BF),
            pltpu.VMEM((SPAN, 1024), BF),
            pltpu.VMEM((SPAN, 1024), BF),
            pltpu.VMEM((4, 4, MSG, 256), BF),
            pltpu.VMEM((2, SPAN, 1024), BF),
            pltpu.VMEM((4, MSG, 256), F32),
            pltpu.VMEM((4, MSG, 256), F32),
            pltpu.VMEM((4, MSG, 256), F32),
            pltpu.VMEM((4, MSG, 256), BF),
            pltpu.VMEM((4, MSG, 256), BF),
            pltpu.VMEM((SPANS, 80, N), BF),
            pltpu.VMEM((SPANS, 80, N), BF),
            pltpu.VMEM((SPANS, 64, N), BF),
            pltpu.VMEM((SPANS, 64, N), BF),
            pltpu.VMEM((SPAN, 1024), F32),
            pltpu.VMEM((SPAN, 1024), F32),
            pltpu.VMEM((MSG, 256), BF),
            pltpu.VMEM((2, 4, MSG, 256), BF),
            pltpu.VMEM((4, 4, 256, 256), BF),
            pltpu.VMEM((3, 4, 128, 256), BF),
            pltpu.VMEM((3, 4, 128, 256), BF),
            pltpu.VMEM((2, 4, 128, 256), BF),
            pltpu.VMEM((2, 3, 128, 256), BF),
            pltpu.VMEM((2, 128, 256), BF),
            pltpu.VMEM((4, SPAN, 256), BF),
            pltpu.VMEM((4, SPAN, 256), BF),
            dma((20 * len(PIECES),)),
            dma((20 * len(PIECES),)),
            dma((8,)),
            dma((8,)),
            dma((2, SPANS)),
            dma((2, SPANS)),
            dma((16,)),
            dma((16,)),
            dma((56,)),
            dma((56,)),
            dma((13,)),
            pltpu.SemaphoreType.REGULAR,
        ],
        compiler_params=pltpu.CompilerParams(collective_id=0, has_side_effects=True),
    )(rows, steps, features, x, u, bias, rate, skip)


def finish_kernel(*refs):
    sources, targets, held, news = refs[:7], refs[7:13], refs[13:20], refs[20:23]
    rows, arrived, stored = refs[23:]
    loads = [
        pltpu.make_async_copy(src, dst, arrived.at[k])
        for k, (src, dst) in enumerate(zip(sources, held))
    ]
    stores = [
        pltpu.make_async_copy(src, dst, stored.at[k])
        for k, (src, dst) in enumerate(zip((*held[4:], *news), targets))
    ]
    for copy in loads:
        copy.start()
    sum_ref, w_ref, fisher_ref, imp_ref = held[:4]
    for k in range(4):
        loads[k].wait()
    for half in (0, 1):
        total = sum_ref[half].astype(F32)
        for k in (0, 1):
            rows[pl.ds(256 * half + k, 128, stride=2), :] = total[:, N * k : N * (k + 1)]
    for k in range(3):
        loads[4 + k].wait()
        stores[k].start()
    grad = rows[...] / TOKENS
    fisher_new = MIX * grad * grad + (1.0 - MIX) * fisher_ref[...]
    delta = -STEP * grad
    news[0][...] = w_ref[...].astype(F32) + delta
    news[1][...] = fisher_new
    news[2][...] = imp_ref[...] + -grad * delta / (0.5 * fisher_new * delta * delta + EPS)
    for copy in stores[3:]:
        copy.start()
    for copy in stores:
        copy.wait()


def finish(y, dx, gf, total, w, fisher, importance):
    wide_out = jax.ShapeDtypeStruct((SPAN, 1024), BF)
    row_out = jax.ShapeDtypeStruct((512, N), F32)
    sources = (total, w, fisher, importance, y, dx, gf)
    return pl.pallas_call(
        finish_kernel,
        name="finish",
        out_shape=(wide_out,) * 3 + (row_out,) * 3,
        in_specs=[ANY] * 7,
        out_specs=(ANY,) * 6,
        scratch_shapes=[pltpu.VMEM(v.shape, v.dtype) for v in sources]
        + [pltpu.VMEM((512, N), F32)] * 4
        + [pltpu.SemaphoreType.DMA((7,)), pltpu.SemaphoreType.DMA((6,))],
    )(*sources)


def local(features, inner, w_bc, w_dt, dt_bias, decay_rate, skip, cotangent, fisher, importance):
    bias, rate, gain = (v.reshape(1, HEADS) for v in (dt_bias, decay_rate, skip))
    rows, fisher_rows, importance_rows = (v.reshape(512, N) for v in (w_bc, fisher, importance))
    outputs, grad_inner, grad_features, total = layer(
        rows, w_dt.T, features, inner, cotangent, bias, rate, gain
    )
    *wides, weight_new, fisher_new, importance_new = finish(
        outputs, grad_inner, grad_features, total, rows, fisher_rows, importance_rows
    )
    news = (v.reshape(w_bc.shape) for v in (weight_new, fisher_new, importance_new))
    return (*wides, *news)


def solution(mesh):
    split = Mesh(mesh.devices.reshape(4, 4, 2, 4, 2), AXES)
    placed = (
        P(CTX, TP),
        P(CTX, TP),
        P(CTX, None, TP),
        P(CTX, TP),
        P(TP),
        P(TP),
        P(TP),
        P(CTX, TP),
        P(CTX, None, TP),
        P(CTX, None, TP),
    )
    return jax.shard_map(
        local,
        mesh=split,
        in_specs=placed,
        out_specs=(
            P(CTX, TP),
            P(CTX, TP),
            P(CTX, TP),
            P(CTX, None, TP),
            P(CTX, None, TP),
            P(CTX, None, TP),
        ),
        check_vma=False,
    )
```
